512 devices in a mesh: ctx: 256 (over z, y, x), head: 2 (over core).
Axes of the slice: x: 4, y: 8, z: 8, core: 2. Of those that a mesh axis runs over, the one named last changes fastest.
Arguments:
- queries: bfloat16 [65536, 8192], P(('ctx', 'head')), may hold values from -64 to 64
- keys: bfloat16 [65536, 1024], P(('ctx', 'head')), may hold values from -64 to 64
- values: bfloat16 [65536, 1024], P(('ctx', 'head')), may hold values from -6 to 6
- doc_lengths: int32 [192], replicated, may hold values from 1 to 1024, as said below
Outputs:
- attended: bfloat16 [65536, 8192], P(('ctx', 'head'))
The draws below stay inside these ranges and needn't reach their ends.
Inputs may be any that keep to these rules, and one draw needn't show every extreme that they name: `doc_lengths`: the lengths sum to 65536; the first document has one token, the second exactly 1024, and no other more than 1024.
All inputs are finite; a program needn't handle non-finite values.
Results may differ from the reference program's by a relative error of at most 0.004.
Values may be sent and summed in bfloat16 or wider, within the bound.
A program may use at most 64 MiB of HBM per device.

```python
import jax
import jax.numpy as jnp
from jax import lax

H = 64
KVH = 8
HD = 128
REACH = 4
SPAN = 256
SEQ = 65536
DOCS = 192
MOST = 1024


def draw_queries(key, part):
    drawn = jnp.clip(jax.random.normal(jax.random.fold_in(key, 1), (SEQ, H * HD), jnp.float32), -6.0, 6.0)
    return drawn.astype(jnp.bfloat16)


def draw_keys(key, part):
    drawn = jnp.clip(jax.random.normal(jax.random.fold_in(key, 2), (SEQ, KVH * HD), jnp.float32), -6.0, 6.0)
    return drawn.astype(jnp.bfloat16)


def draw_doc_lengths(key, part):
    count = DOCS - 2
    remaining = SEQ - MOST - 1
    index_list = jnp.arange(count, dtype=jnp.int32)
    lengths = (remaining // count + (index_list < remaining % count).astype(jnp.int32)).astype(jnp.int32)
    half = count // 2
    for round_number in range(8):
        round_key = jax.random.fold_in(key, 100 + round_number)
        order = jax.random.permutation(jax.random.fold_in(round_key, 1), count)
        left = order[:half]
        right = order[half:2 * half]
        room = jnp.minimum(MOST - lengths[left], lengths[right] - 1)
        fraction = jax.random.randint(jax.random.fold_in(round_key, 2), (half,), 0, 1001, dtype=jnp.int32)
        moved = room * fraction // 1000
        lengths = lengths.at[left].add(moved).at[right].add(-moved)
    head_part = jnp.array([1, MOST], dtype=jnp.int32)
    return jnp.concatenate([head_part, lengths.astype(jnp.int32)]).astype(jnp.int32)


def level_of(stream_key, dims, pieces, least, top_value):
    gain, own = 1.0, jax.random.fold_in(stream_key, 6)
    for axis_at, parts in pieces:
        draws = jnp.exp(jax.random.uniform(jax.random.fold_in(own, axis_at), (parts,), jnp.float32, least / len(pieces), top_value / len(pieces)))
        gain = gain * jnp.repeat(draws, dims[axis_at] // parts).reshape([-1 if axis == axis_at else 1 for axis in range(len(dims))])
    return gain


def centred(own_key, extent, scale, bound, pieces=(), kind=jnp.bfloat16):
    entries = scale * jax.random.normal(own_key, extent, jnp.float32)
    if pieces:
        entries = entries * level_of(own_key, extent, pieces, -0.22, 0.18)
    return jnp.clip(entries, -bound, bound).astype(kind)


def setup_inputs(seed: int = 0) -> dict:
    key_of = jax.random.split(jax.random.key(seed), 5)
    return {
        "queries": draw_queries(jax.random.fold_in(key_of[4], 71), 0),
        "keys": draw_keys(jax.random.fold_in(key_of[4], 71), 0),
        "values": centred(key_of[2], (SEQ, KVH * HD), 1.0, 6.0, ((0, 512),)),
        "doc_lengths": draw_doc_lengths(jax.random.fold_in(key_of[4], 71), 0),
    }


def doc_index(positions, doc_ends):
    return jnp.sum((doc_ends[None, :] <= positions[:, None]).astype(jnp.int32), axis=1)


def reference(queries, keys, values, doc_lengths):
    doc_ends = jnp.cumsum(doc_lengths).astype(jnp.int32)
    group_size = H // KVH
    query_rows = min(256, SPAN)
    padding = REACH * SPAN
    window = padding + query_rows
    score_scale = HD ** -0.5
    keys_padded = jnp.concatenate([jnp.zeros((padding, KVH * HD), keys.dtype), keys], axis=0)
    values_padded = jnp.concatenate([jnp.zeros((padding, KVH * HD), values.dtype), values], axis=0)

    def one_block(block_index):
        offset = (block_index * query_rows).astype(jnp.int32)
        query_block = lax.dynamic_slice_in_dim(queries, offset, query_rows, 0)
        query_block = query_block.reshape(query_rows, KVH, group_size, HD).astype(jnp.float32)
        key_block = lax.dynamic_slice_in_dim(keys_padded, offset, window, 0)
        key_block = key_block.reshape(window, KVH, HD).astype(jnp.float32)
        value_block = lax.dynamic_slice_in_dim(values_padded, offset, window, 0)
        value_block = value_block.reshape(window, KVH, HD).astype(jnp.float32)
        query_pos = offset + jnp.arange(query_rows, dtype=jnp.int32)
        key_pos = offset - padding + jnp.arange(window, dtype=jnp.int32)
        allowed = (doc_index(query_pos, doc_ends)[:, None] == doc_index(key_pos, doc_ends)[None, :])
        allowed = allowed & (key_pos[None, :] <= query_pos[:, None]) & (key_pos[None, :] >= 0)
        wide = allowed[:, None, None, :]
        scores = jnp.einsum('qkgd,skd->qkgs', query_block, key_block) * score_scale
        row_max = jnp.max(jnp.where(wide, scores, jnp.float32(-1e30)), axis=-1, keepdims=True)
        weights = jnp.where(wide, jnp.exp(scores - row_max), jnp.float32(0.0))
        row_sum = jnp.sum(weights, axis=-1)
        rounded = lax.optimization_barrier(weights.astype(jnp.bfloat16)).astype(jnp.float32)
        output = jnp.einsum('qkgs,skd->qkgd', rounded, value_block) / row_sum[..., None]
        return output.reshape(query_rows, H * HD).astype(jnp.bfloat16)

    blocks = lax.map(one_block, jnp.arange(SEQ // query_rows, dtype=jnp.int32))
    return blocks.reshape(SEQ, H * HD)
```

```python
import math

import jax
import jax.numpy as jnp
from jax import lax
from jax.experimental import pallas as pl
from jax.experimental.pallas import tpu as pltpu
from jax.sharding import PartitionSpec as P

H = 64
KVH = 8
HD = 128
GROUP = H // KVH
ROW = 4
BACK = 4
BLOCKS = 2 * (BACK + 1)
WINDOW = 2 * BACK + 1
T = 128
PAIR = 2
BIG = float(2**24)
MESH = pl.DeviceIdType.MESH


def kernel(
    lens_ref, q_hbm, k_hbm, v_hbm, out_ref,
    q_ref, buf, fk_ref, fq_ref, bias_ref, q_sem, kv_sem, ssem, rsem,
):
    c = lax.axis_index("ctx")
    i = lax.axis_index("head")
    n = lax.axis_size("ctx")
    x = c % ROW
    first = (c // ROW) * ROW
    right = (first + (x + 1) % ROW, i)
    left = (first + (x + ROW - 1) % ROW, i)
    up = ((c + ROW) % n, i)
    down = ((c + n - ROW) % n, i)
    partner = (c, 1 - i)
    middle = ((x + 1) // 2) % 2 == 1

    def block(slot):
        return 2 * (BACK - slot) + i

    def own_k(h):
        return pltpu.make_async_copy(
            k_hbm.at[:, pl.ds(pl.multiple_of(h * HD, HD), HD)], buf.at[h, block(0), 0], kv_sem.at[h, 0]
        )

    def own_v(h):
        return pltpu.make_async_copy(
            v_hbm.at[:, pl.ds(pl.multiple_of(h * HD, HD), HD)], buf.at[h, block(0), 1], kv_sem.at[h, 1]
        )

    q_copy = pltpu.make_async_copy(q_hbm, q_ref, q_sem)

    def send(h, src, dst, s, r, device):
        return pltpu.make_async_remote_copy(
            src_ref=buf.at[h, src],
            dst_ref=buf.at[h, dst],
            send_sem=ssem.at[h, s],
            recv_sem=rsem.at[h, r],
            device_id=device,
            device_id_type=MESH,
        )

    def to_up(h):
        return send(h, block(0), block(BACK), 0, BACK, up)

    def to_right(h):
        return send(h, i + 8 * (1 - (x + 1) // ROW), block(1), 1, 1, right)

    def to_left(h):
        return send(h, i + 8 * ((ROW - 1 - x) // (ROW - 1)), block(3), 3, 3, left)

    def relay_right(h):
        return send(h, block(1), block(2), 2, 2, right)

    def relay_left(h):
        return send(h, block(3), block(2), 9, 2, left)

    def share(h, slot):
        return send(h, block(slot), block(slot), 4 + slot, 5 + slot, partner)

    def arrived(h, slot):
        send(h, block(slot), block(slot), 0, slot, partner).wait_recv()

    def shared(h, slot):
        other = 2 * (BACK - slot) + 1 - i
        send(h, other, other, 0, 5 + slot, partner).wait_recv()

    def stage1(h):
        arrived(h, 4)
        to_left(h).start()
        to_right(h).start()
        share(h, 4).start()

    def stage2(h):
        arrived(h, 1)
        arrived(h, 3)

        @pl.when(middle)
        def _():
            relay_left(h).start()
            relay_right(h).start()

        share(h, 1).start()
        share(h, 3).start()

    def stage3(h):
        arrived(h, 2)
        share(h, 2).start()

    for h in range(KVH):
        own_k(h).start()
        own_v(h).start()
    barrier = pltpu.get_barrier_semaphore()
    for device in (up, down, left, right, partner):
        pl.semaphore_signal(barrier, inc=1, device_id=device, device_id_type=MESH)
    pl.semaphore_wait(barrier, 5)
    for h in range(KVH):
        own_k(h).wait()
        own_v(h).wait()
        to_up(h).start()
    for h in range(KVH):
        share(h, 0).start()
    q_copy.start()

    docs = lens_ref.shape[1]
    lens = lens_ref[...].astype(jnp.float32)
    ia = lax.broadcasted_iota(jnp.int32, (docs, docs), 0)
    ib = lax.broadcasted_iota(jnp.int32, (docs, docs), 1)
    column = jnp.sum(jnp.where(ia == ib, lens, 0.0), axis=1, keepdims=True)
    ends = jnp.sum(jnp.where(ia <= ib, column, 0.0), axis=0, keepdims=True)
    begin = c * (2 * T) + i * T - (WINDOW - 1) * T
    position = begin + lax.broadcasted_iota(jnp.int32, (WINDOW * T, 1), 0)
    before = (ends <= position.astype(jnp.float32)).astype(jnp.float32)
    doc = jnp.sum(before, axis=1, keepdims=True)
    doc = doc - doc[(WINDOW - 1) * T:(WINDOW - 1) * T + 1, :]
    lane = lax.broadcasted_iota(jnp.int32, (WINDOW * T, T), 1).astype(jnp.float32)
    same = (doc == lane) & (position >= 0)
    fk_ref[...] = jnp.where(same, 0.0, 1.0).astype(jnp.bfloat16)
    fq_ref[...] = jnp.where(same[(WINDOW - 1) * T:], -BIG, 0.0).astype(jnp.bfloat16)
    row = lax.broadcasted_iota(jnp.int32, (PAIR * T, T), 0) % T
    col = lax.broadcasted_iota(jnp.int32, (PAIR * T, T), 1)
    bias_ref[...] = jnp.where(col <= row, 0.0, -BIG)

    def compute(h):
        keys = buf[h, pl.ds(i, WINDOW), 0].reshape(WINDOW * T, HD)
        values = buf[h, pl.ds(i, WINDOW), 1].reshape(WINDOW * T, HD)
        keys = jnp.concatenate([keys, fk_ref[...]], axis=1)
        values = jnp.concatenate([values, jnp.ones((WINDOW * T, HD), jnp.bfloat16)], axis=1)
        factor = jnp.float32(HD**-0.5 * math.log2(math.e))
        for pair in range(GROUP // PAIR):
            at = [pl.multiple_of((h * GROUP + pair * PAIR + g) * HD, HD) for g in range(PAIR)]
            q = jnp.concatenate(
                [jnp.concatenate([q_ref[:, pl.ds(a, HD)], fq_ref[...]], axis=1) for a in at], axis=0
            )
            s = lax.dot_general(q, keys, (((1,), (1,)), ((), ())), preferred_element_type=jnp.float32)
            far, near = s[:, :(WINDOW - 1) * T], s[:, (WINDOW - 1) * T:] + bias_ref[...]
            s = jnp.concatenate([far, near], axis=1)
            top = jnp.max(s, axis=1, keepdims=True)
            w = jnp.exp2((s - top) * factor).astype(jnp.bfloat16)
            o = jnp.dot(w, values, preferred_element_type=jnp.float32)
            o = (o[:, :HD] / o[:, HD:]).astype(jnp.bfloat16)
            for g in range(PAIR):
                out_ref[:, pl.ds(at[g], HD)] = o[g * T:(g + 1) * T]

    for h in range(3):
        stage1(h)
    stage2(0)
    stage1(3)
    stage2(1)
    stage3(0)
    q_copy.wait()

    @pl.loop(0, KVH)
    def _(h):
        @pl.when(h + 4 < KVH)
        def _():
            stage1(h + 4)

        @pl.when(h + 2 < KVH)
        def _():
            stage2(h + 2)

        @pl.when(h + 1 < KVH)
        def _():
            stage3(h + 1)

        for slot in range(BACK + 1):
            shared(h, slot)
        compute(h)

    @pl.loop(0, KVH)
    def _(h):
        to_up(h).wait_send()
        to_right(h).wait_send()
        to_left(h).wait_send()
        for slot in range(BACK + 1):
            share(h, slot).wait_send()

        @pl.when(middle)
        def _():
            relay_left(h).wait_send()
            relay_right(h).wait_send()


def per_device(queries, keys, values, doc_lengths):
    any_space = pl.BlockSpec(memory_space=pl.ANY)
    vmem = pl.BlockSpec(memory_space=pltpu.VMEM)
    return pl.pallas_call(
        kernel,
        out_shape=jax.ShapeDtypeStruct(queries.shape, queries.dtype),
        in_specs=[vmem, any_space, any_space, any_space],
        out_specs=vmem,
        scratch_shapes=[
            pltpu.VMEM((T, H * HD), jnp.bfloat16),
            pltpu.VMEM((KVH, BLOCKS, 2, T, HD), jnp.bfloat16),
            pltpu.VMEM((WINDOW * T, HD), jnp.bfloat16),
            pltpu.VMEM((T, HD), jnp.bfloat16),
            pltpu.VMEM((PAIR * T, T), jnp.float32),
            pltpu.SemaphoreType.DMA,
            pltpu.SemaphoreType.DMA((KVH, 2)),
            pltpu.SemaphoreType.DMA((KVH, 10)),
            pltpu.SemaphoreType.DMA((KVH, 10)),
        ],
        compiler_params=pltpu.CompilerParams(collective_id=0, has_side_effects=True),
    )(doc_lengths.reshape(1, -1), queries, keys, values)


def solution(mesh):
    placed = (P(("ctx", "head"), None), P(("ctx", "head"), None), P(("ctx", "head"), None), P())
    return jax.shard_map(
        per_device, mesh=mesh, in_specs=placed, out_specs=P(("ctx", "head"), None), check_vma=False
    )
```

```python
import math

import jax
import jax.numpy as jnp
from jax import lax
from jax.experimental import pallas as pl
from jax.experimental.pallas import tpu as pltpu
from jax.sharding import PartitionSpec as P

H = 64
KVH = 8
HD = 128
GROUP = H // KVH
ROW = 4
BACK = 4
BLOCKS = 2 * (BACK + 1)
WINDOW = 2 * BACK + 1
T = 128
PAIR = 2
BIG = float(2**24)
MESH = pl.DeviceIdType.MESH


def kernel(
    lens_hbm, q_hbm, k_hbm, v_hbm, out_ref,
    lens_ref, q_ref, buf, fk_ref, fq_ref, bias_ref, lens_sem, q_sem, kv_sem, ssem, rsem,
):
    c = lax.axis_index("ctx")
    i = lax.axis_index("head")
    n = lax.axis_size("ctx")
    x = c % ROW
    first = (c // ROW) * ROW
    right = (first + (x + 1) % ROW, i)
    left = (first + (x + ROW - 1) % ROW, i)
    up = ((c + ROW) % n, i)
    down = ((c + n - ROW) % n, i)
    partner = (c, 1 - i)
    across = (first + (x + 2) % ROW, i)
    has_down = c >= ROW
    has_up = c < n - ROW

    def block(slot):
        return 2 * (BACK - slot) + i

    def own(h, which, slot=0):
        source = (k_hbm, v_hbm)[which].at[:, pl.ds(pl.multiple_of(h * HD, HD), HD)]
        return pltpu.make_async_copy(source, buf.at[h, block(slot), which], kv_sem.at[h, which + slot // 2])

    q_copy = pltpu.make_async_copy(q_hbm, q_ref, q_sem)
    lens_copy = pltpu.make_async_copy(lens_hbm, lens_ref, lens_sem)

    def send(h, src, dst, s, r, device):
        return pltpu.make_async_remote_copy(
            src_ref=buf.at[h, src],
            dst_ref=buf.at[h, dst],
            send_sem=ssem.at[h, s],
            recv_sem=rsem.at[h, r],
            device_id=device,
            device_id_type=MESH,
        )

    def to_up(h):
        return send(h, block(0), block(BACK), 0, BACK, up)

    def to_right(h):
        return send(h, i + 8 * (1 - (x + 1) // ROW), block(1), 1, 1, right)

    def to_left(h):
        return send(h, i + 8 * ((ROW - 1 - x) // (ROW - 1)), block(3), 3, 3, left)

    def to_across(h):
        return send(h, i + 8 * (1 - x // 2), block(2), 2, 2, across)

    def share(h, slot):
        return send(h, block(slot), block(slot), 4 + slot, 5 + slot, partner)

    def arrived(h, slot):
        send(h, block(slot), block(slot), 0, slot, partner).wait_recv()

    def shared(h, slot):
        other = 2 * (BACK - slot) + 1 - i
        send(h, other, other, 0, 5 + slot, partner).wait_recv()

    def stage1(h):
        @pl.when(has_down)
        def _():
            arrived(h, 4)

        to_left(h).start()
        to_right(h).start()
        to_across(h).start()
        share(h, 4).start()

    def stage2(h):
        for slot in (1, 3, 2):
            arrived(h, slot)
            share(h, slot).start()

    for h in range(KVH):
        own(h, 0).start()
        own(h, 1).start()
    lens_copy.start()
    barrier = pltpu.get_barrier_semaphore()
    for device in (left, right, across, partner):
        pl.semaphore_signal(barrier, inc=1, device_id=device, device_id_type=MESH)

    @pl.when(has_down)
    def _():
        pl.semaphore_signal(barrier, inc=1, device_id=down, device_id_type=MESH)

    @pl.when(has_up)
    def _():
        pl.semaphore_signal(barrier, inc=1, device_id=up, device_id_type=MESH)

    @pl.when(c < ROW)
    def _():
        for h in range(KVH):
            own(h, 0, BACK).start()
            own(h, 1, BACK).start()
        for h in range(KVH):
            own(h, 0, BACK).wait()
            own(h, 1, BACK).wait()

    pl.semaphore_wait(barrier, 4 + jnp.minimum(c // ROW, 1) + jnp.minimum((n - 1 - c) // ROW, 1))
    for h in range(KVH):
        own(h, 0).wait()
        own(h, 1).wait()

        @pl.when(has_up)
        def _():
            to_up(h).start()

    for h in range(KVH):
        share(h, 0).start()
    q_copy.start()

    lens_copy.wait()
    docs = lens_ref.shape[1]
    lens = lens_ref[...].astype(jnp.float32)
    ia = lax.broadcasted_iota(jnp.int32, (docs, docs), 0)
    ib = lax.broadcasted_iota(jnp.int32, (docs, docs), 1)
    column = jnp.sum(jnp.where(ia == ib, lens, 0.0), axis=1, keepdims=True)
    ends = jnp.sum(jnp.where(ia <= ib, column, 0.0), axis=0, keepdims=True)
    begin = c * (2 * T) + i * T - (WINDOW - 1) * T
    position = begin + lax.broadcasted_iota(jnp.int32, (WINDOW * T, 1), 0)
    before = (ends <= position.astype(jnp.float32)).astype(jnp.float32)
    doc = jnp.sum(before, axis=1, keepdims=True)
    doc = doc - doc[(WINDOW - 1) * T:(WINDOW - 1) * T + 1, :]
    lane = lax.broadcasted_iota(jnp.int32, (WINDOW * T, T), 1).astype(jnp.float32)
    same = (doc == lane) & (position >= 0)
    fk_ref[...] = jnp.where(same, 0.0, 1.0).astype(jnp.bfloat16)
    fq_ref[...] = jnp.where(same[(WINDOW - 1) * T:], -BIG, 0.0).astype(jnp.bfloat16)
    row = lax.broadcasted_iota(jnp.int32, (PAIR * T, T), 0) % T
    col = lax.broadcasted_iota(jnp.int32, (PAIR * T, T), 1)
    bias_ref[...] = jnp.where(col <= row, 0.0, -BIG)

    def compute(h):
        keys = buf[h, pl.ds(i, WINDOW), 0].reshape(WINDOW * T, HD)
        values = buf[h, pl.ds(i, WINDOW), 1].reshape(WINDOW * T, HD)
        keys = jnp.concatenate([keys, fk_ref[...]], axis=1)
        values = jnp.concatenate([values, jnp.ones((WINDOW * T, HD), jnp.bfloat16)], axis=1)
        factor = jnp.float32(HD**-0.5 * math.log2(math.e))
        for pair in range(GROUP // PAIR):
            at = [pl.multiple_of((h * GROUP + pair * PAIR + g) * HD, HD) for g in range(PAIR)]
            q = jnp.concatenate(
                [jnp.concatenate([q_ref[:, pl.ds(a, HD)], fq_ref[...]], axis=1) for a in at], axis=0
            )
            s = lax.dot_general(q, keys, (((1,), (1,)), ((), ())), preferred_element_type=jnp.float32)
            far, near = s[:, :(WINDOW - 1) * T], s[:, (WINDOW - 1) * T:] + bias_ref[...]
            s = jnp.concatenate([far, near], axis=1)
            top = jnp.max(s, axis=1, keepdims=True)
            w = jnp.exp2((s - top) * factor).astype(jnp.bfloat16)
            o = jnp.dot(w, values, preferred_element_type=jnp.float32)
            o = (o[:, :HD] / o[:, HD:]).astype(jnp.bfloat16)
            for g in range(PAIR):
                out_ref[:, pl.ds(at[g], HD)] = o[g * T:(g + 1) * T]

    for h in range(4):
        stage1(h)
    stage2(0)
    q_copy.wait()

    @pl.loop(0, KVH)
    def _(h):
        @pl.when(h + 4 < KVH)
        def _():
            stage1(h + 4)

        @pl.when(h + 1 < KVH)
        def _():
            stage2(h + 1)

        for slot in range(BACK + 1):
            shared(h, slot)
        compute(h)

    @pl.loop(0, KVH)
    def _(h):
        @pl.when(has_up)
        def _():
            to_up(h).wait_send()

        to_right(h).wait_send()
        to_left(h).wait_send()
        to_across(h).wait_send()
        for slot in range(BACK + 1):
            share(h, slot).wait_send()


def per_device(queries, keys, values, doc_lengths):
    hbm = pl.BlockSpec(memory_space=pltpu.HBM)
    vmem = pl.BlockSpec(memory_space=pltpu.VMEM)
    lengths = doc_lengths.reshape(1, -1)
    operands = [pltpu.with_memory_space_constraint(a, pltpu.HBM) for a in (lengths, queries, keys, values)]
    return pl.pallas_call(
        kernel,
        out_shape=jax.ShapeDtypeStruct(queries.shape, queries.dtype),
        in_specs=[hbm, hbm, hbm, hbm],
        out_specs=vmem,
        scratch_shapes=[
            pltpu.VMEM((1, doc_lengths.shape[0]), jnp.int32),
            pltpu.VMEM((T, H * HD), jnp.bfloat16),
            pltpu.VMEM((KVH, BLOCKS, 2, T, HD), jnp.bfloat16),
            pltpu.VMEM((WINDOW * T, HD), jnp.bfloat16),
            pltpu.VMEM((T, HD), jnp.bfloat16),
            pltpu.VMEM((PAIR * T, T), jnp.float32),
            pltpu.SemaphoreType.DMA,
            pltpu.SemaphoreType.DMA,
            pltpu.SemaphoreType.DMA((KVH, 4)),
            pltpu.SemaphoreType.DMA((KVH, 10)),
            pltpu.SemaphoreType.DMA((KVH, 10)),
        ],
        compiler_params=pltpu.CompilerParams(collective_id=0, has_side_effects=True, vmem_limit_bytes=24 << 20),
    )(*operands)


def solution(mesh):
    placed = (P(("ctx", "head"), None), P(("ctx", "head"), None), P(("ctx", "head"), None), P())
    return jax.shard_map(
        per_device, mesh=mesh, in_specs=placed, out_specs=P(("ctx", "head"), None), check_vma=False
    )
```

```python
import math

import jax
import jax.numpy as jnp
from jax import lax
from jax.experimental import pallas as pl
from jax.experimental.pallas import tpu as pltpu
from jax.sharding import PartitionSpec as P

H = 64
KVH = 8
HD = 128
GROUP = H // KVH
ROW = 4
BACK = 4
BLOCKS = 2 * (BACK + 1)
WINDOW = 2 * BACK + 1
T = 128
PAIR = 2
UNITS = GROUP // PAIR
STEPS = UNITS // 2
EARLY = 3
BIG = float(2**24)
MESH = pl.DeviceIdType.MESH


def kernel(
    lens_hbm, q_hbm, k_hbm, v_hbm, out_ref,
    lens_ref, q_ref, buf, fk_ref, fq_ref, bias_ref, s_a, s_b, w_a, w_b, lens_sem, q_sem, kv_sem, ssem, rsem,
):
    c = lax.axis_index("ctx")
    i = lax.axis_index("head")
    n = lax.axis_size("ctx")
    x = c % ROW
    first = (c // ROW) * ROW
    right = (first + (x + 1) % ROW, i)
    left = (first + (x + ROW - 1) % ROW, i)
    up = ((c + ROW) % n, i)
    down = ((c + n - ROW) % n, i)
    partner = (c, 1 - i)
    across = (first + (x + 2) % ROW, i)
    has_down = c >= ROW
    has_up = c < n - ROW

    def block(slot):
        return 2 * (BACK - slot) + i

    def own(h, which, slot=0):
        source = (k_hbm, v_hbm)[which].at[:, pl.ds(pl.multiple_of(h * HD, HD), HD)]
        return pltpu.make_async_copy(source, buf.at[h, block(slot), which], kv_sem.at[h, which + slot // 2])

    q_copy = pltpu.make_async_copy(q_hbm, q_ref, q_sem)
    lens_copy = pltpu.make_async_copy(lens_hbm, lens_ref, lens_sem)

    def send(h, src, dst, s, r, device, which=None):
        return pltpu.make_async_remote_copy(
            src_ref=buf.at[h, src] if which is None else buf.at[h, src, which],
            dst_ref=buf.at[h, dst] if which is None else buf.at[h, dst, which],
            send_sem=ssem.at[h, s],
            recv_sem=rsem.at[h, r],
            device_id=device,
            device_id_type=MESH,
        )

    def to_up(h):
        return send(h, block(0), block(BACK), 0, BACK, up)

    def to_right(h):
        return send(h, i + 8 * (1 - (x + 1) // ROW), block(1), 1, 1, right)

    def to_left(h):
        return send(h, i + 8 * ((ROW - 1 - x) // (ROW - 1)), block(3), 3, 3, left)

    sends_across = (x == 1) | (x == 2)
    relays_right = x < ROW - 1
    relays_left = x > 0
    passes = 1 - x // 2

    def to_across(h):
        return send(h, i + 8 * (1 - x // 2), block(2), 2, 2, across, 0)

    def relay_right(h):
        return send(h, block(1), block(2), 9, 10, right, 1)

    def relay_left(h):
        return send(h, block(3), block(2), 10, 2 + 8 * passes, left, passes)

    def share(h, slot):
        return send(h, block(slot), block(slot), 4 + slot, 5 + slot, partner)

    def arrived(h, slot):
        send(h, block(slot), block(slot), 0, slot, partner).wait_recv()

    def shared(h, slot):
        other = 2 * (BACK - slot) + 1 - i
        send(h, other, other, 0, 5 + slot, partner).wait_recv()

    def stage1(h, ahead):
        @pl.when(has_down)
        def _():
            arrived(h, 4)

        to_left(h).start()

        @pl.when(x == ROW - 1)
        def _():
            to_right(h).start()

        @pl.when(x == 2)
        def _():
            to_across(h).start()

        share(h, 4).start()

        @pl.when((x < ROW - 1) & ahead)
        def _():
            to_right(jnp.minimum(h + EARLY, KVH - 1)).start()

    def stage2(h):
        arrived(h, 1)

        @pl.when(relays_right)
        def _():
            relay_right(h).start()

        arrived(h, 3)

        @pl.when(relays_left)
        def _():
            relay_left(h).start()

        share(h, 1).start()
        share(h, 3).start()

    def stage3(h):
        send(h, block(2), block(2), 0, 2, partner, 0).wait_recv()
        send(h, block(2), block(2), 0, 10, partner, 1).wait_recv()
        share(h, 2).start()

    for h in range(KVH):
        own(h, 0).start()
        own(h, 1).start()
    lens_copy.start()
    barrier = pltpu.get_barrier_semaphore()
    for device in (left, right, across, partner):
        pl.semaphore_signal(barrier, inc=1, device_id=device, device_id_type=MESH)

    @pl.when(has_down)
    def _():
        pl.semaphore_signal(barrier, inc=1, device_id=down, device_id_type=MESH)

    @pl.when(has_up)
    def _():
        pl.semaphore_signal(barrier, inc=1, device_id=up, device_id_type=MESH)

    @pl.when(c < ROW)
    def _():
        for h in range(KVH):
            own(h, 0, BACK).start()
            own(h, 1, BACK).start()
        for h in range(KVH):
            own(h, 0, BACK).wait()
            own(h, 1, BACK).wait()

    pl.semaphore_wait(barrier, 4 + jnp.minimum(c // ROW, 1) + jnp.minimum((n - 1 - c) // ROW, 1))
    for h in range(KVH):
        own(h, 0).wait()
        own(h, 1).wait()

        @pl.when(has_up)
        def _():
            to_up(h).start()

    @pl.when(x < ROW - 1)
    def _():
        for h in range(EARLY):
            to_right(h).start()

    @pl.when(x == 1)
    def _():
        for h in range(KVH):
            to_across(h).start()

    for h in range(KVH):
        share(h, 0).start()
    q_copy.start()

    lens_copy.wait()
    docs = lens_ref.shape[1]
    lens = lens_ref[...].astype(jnp.float32)
    ia = lax.broadcasted_iota(jnp.int32, (docs, docs), 0)
    ib = lax.broadcasted_iota(jnp.int32, (docs, docs), 1)
    column = jnp.sum(jnp.where(ia == ib, lens, 0.0), axis=1, keepdims=True)
    ends = jnp.sum(jnp.where(ia <= ib, column, 0.0), axis=0, keepdims=True)
    begin = c * (2 * T) + i * T - (WINDOW - 1) * T
    position = begin + lax.broadcasted_iota(jnp.int32, (WINDOW * T, 1), 0)
    before = (ends <= position.astype(jnp.float32)).astype(jnp.float32)
    doc = jnp.sum(before, axis=1, keepdims=True)
    doc = doc - doc[(WINDOW - 1) * T:(WINDOW - 1) * T + 1, :]
    lane = lax.broadcasted_iota(jnp.int32, (WINDOW * T, T), 1).astype(jnp.float32)
    same = (doc == lane) & (position >= 0)
    fk_ref[...] = jnp.where(same, 0.0, 1.0).astype(jnp.bfloat16)
    fq_ref[...] = jnp.where(same[(WINDOW - 1) * T:], -BIG, 0.0).astype(jnp.bfloat16)
    row = lax.broadcasted_iota(jnp.int32, (PAIR * T, T), 0) % T
    col = lax.broadcasted_iota(jnp.int32, (PAIR * T, T), 1)
    bias_ref[...] = jnp.where(col <= row, 0.0, -BIG)

    def heads_of(unit):
        return [pl.multiple_of((unit * PAIR + g) * HD, HD) for g in range(PAIR)]

    def window(unit, which):
        return buf[unit // UNITS, pl.ds(i, WINDOW), which].reshape(WINDOW * T, HD)

    def score(unit, s_ref):
        keys = jnp.concatenate([window(unit, 0), fk_ref[...]], axis=1)
        q = jnp.concatenate(
            [jnp.concatenate([q_ref[:, pl.ds(a, HD)], fq_ref[...]], axis=1) for a in heads_of(unit)], axis=0
        )
        s_ref[...] = lax.dot_general(q, keys, (((1,), (1,)), ((), ())), preferred_element_type=jnp.float32)

    def weigh(s_ref, w_ref):
        far, near = s_ref[:, :(WINDOW - 1) * T], s_ref[:, (WINDOW - 1) * T:] + bias_ref[...]
        s = jnp.concatenate([far, near], axis=1)
        top = jnp.max(s, axis=1, keepdims=True)
        w_ref[...] = jnp.exp2((s - top) * jnp.float32(HD**-0.5 * math.log2(math.e))).astype(jnp.bfloat16)

    def attend(unit, w_ref):
        values = jnp.concatenate([window(unit, 1), jnp.ones((WINDOW * T, HD), jnp.bfloat16)], axis=1)
        o = jnp.dot(w_ref[...], values, preferred_element_type=jnp.float32)
        o = (o[:, :HD] / o[:, HD:]).astype(jnp.bfloat16)
        for g, a in enumerate(heads_of(unit)):
            out_ref[:, pl.ds(a, HD)] = o[g * T:(g + 1) * T]

    last = KVH * UNITS - 1

    def clamped(unit):
        return jnp.maximum(unit, 0)

    def two_units(j):
        attend(clamped(2 * j - 2), w_a)
        weigh(s_b, w_b)
        score(2 * j, s_a)
        attend(clamped(2 * j - 1), w_b)
        weigh(s_a, w_a)
        score(2 * j + 1, s_b)

    for h in range(4):
        stage1(h, h + EARLY < KVH)
    stage2(0)
    stage2(1)
    stage3(0)
    q_copy.wait()

    @pl.loop(0, KVH * STEPS)
    def _(j):
        h = j // STEPS

        @pl.when(j % STEPS == 0)
        def _():
            @pl.when(h + 4 < KVH)
            def _():
                stage1(h + 4, h + 4 + EARLY < KVH)

            for slot in range(BACK + 1):
                shared(h, slot)

        @pl.when((j % STEPS == 0) & (h + 2 < KVH))
        def _():
            stage2(h + 2)

        @pl.when((j % STEPS == STEPS - 1) & (h + 1 < KVH))
        def _():
            stage3(h + 1)

        two_units(j)

    attend(last - 1, w_a)
    weigh(s_b, w_b)
    attend(last, w_b)

    @pl.loop(0, KVH)
    def _(h):
        @pl.when(has_up)
        def _():
            to_up(h).wait_send()

        to_right(h).wait_send()
        to_left(h).wait_send()
        for slot in range(BACK + 1):
            share(h, slot).wait_send()

        @pl.when(sends_across)
        def _():
            to_across(h).wait_send()

        @pl.when(relays_right)
        def _():
            relay_right(h).wait_send()

        @pl.when(relays_left)
        def _():
            relay_left(h).wait_send()


def per_device(queries, keys, values, doc_lengths):
    hbm = pl.BlockSpec(memory_space=pltpu.HBM)
    vmem = pl.BlockSpec(memory_space=pltpu.VMEM)
    lengths = doc_lengths.reshape(1, -1)
    operands = [pltpu.with_memory_space_constraint(a, pltpu.HBM) for a in (lengths, queries, keys, values)]
    return pl.pallas_call(
        kernel,
        out_shape=jax.ShapeDtypeStruct(queries.shape, queries.dtype),
        in_specs=[hbm, hbm, hbm, hbm],
        out_specs=vmem,
        scratch_shapes=[
            pltpu.VMEM((1, doc_lengths.shape[0]), jnp.int32),
            pltpu.VMEM((T, H * HD), jnp.bfloat16),
            pltpu.VMEM((KVH, BLOCKS, 2, T, HD), jnp.bfloat16),
            pltpu.VMEM((WINDOW * T, HD), jnp.bfloat16),
            pltpu.VMEM((T, HD), jnp.bfloat16),
            pltpu.VMEM((PAIR * T, T), jnp.float32),
            pltpu.VMEM((PAIR * T, WINDOW * T), jnp.float32),
            pltpu.VMEM((PAIR * T, WINDOW * T), jnp.float32),
            pltpu.VMEM((PAIR * T, WINDOW * T), jnp.bfloat16),
            pltpu.VMEM((PAIR * T, WINDOW * T), jnp.bfloat16),
            pltpu.SemaphoreType.DMA,
            pltpu.SemaphoreType.DMA,
            pltpu.SemaphoreType.DMA((KVH, 4)),
            pltpu.SemaphoreType.DMA((KVH, 11)),
            pltpu.SemaphoreType.DMA((KVH, 11)),
        ],
        compiler_params=pltpu.CompilerParams(collective_id=0, has_side_effects=True, vmem_limit_bytes=24 << 20),
    )(*operands)


def solution(mesh):
    placed = (P(("ctx", "head"), None), P(("ctx", "head"), None), P(("ctx", "head"), None), P())
    return jax.shard_map(
        per_device, mesh=mesh, in_specs=placed, out_specs=P(("ctx", "head"), None), check_vma=False
    )
```

```python
import math

import jax
import jax.numpy as jnp
from jax import lax
from jax.experimental import pallas as pl
from jax.experimental.pallas import tpu as pltpu
from jax.sharding import PartitionSpec as P

H = 64
KVH = 8
HD = 128
GROUP = H // KVH
ROW = 4
BACK = 4
BLOCKS = 2 * (BACK + 1)
WINDOW = 2 * BACK + 1
T = 128
PAIR = 2
BIG = float(2**24)
MESH = pl.DeviceIdType.MESH


def kernel(
    lens_hbm, q_hbm, k_hbm, v_hbm, out_ref,
    lens_ref, q_ref, buf, fk_ref, fq_ref, bias_ref, lens_sem, q_sem, fill_sem, kv_sem, ssem, rsem,
):
    c = lax.axis_index("ctx")
    i = lax.axis_index("head")
    n = lax.axis_size("ctx")
    x = c % ROW
    first = (c // ROW) * ROW
    right = (first + (x + 1) % ROW, i)
    left = (first + (x + ROW - 1) % ROW, i)
    up = ((c + ROW) % n, i)
    down = ((c + n - ROW) % n, i)
    partner = (c, 1 - i)
    across = (first + (x + 2) % ROW, i)
    has_down = c >= ROW
    has_up = c < n - ROW

    def block(slot):
        return 2 * (BACK - slot) + i

    def own(h, which, slot=0):
        source = (k_hbm, v_hbm)[which].at[:, pl.ds(pl.multiple_of(h * HD, HD), HD)]
        return pltpu.make_async_copy(source, buf.at[h, block(slot), which], fill_sem if slot else kv_sem.at[h])

    q_copy = pltpu.make_async_copy(q_hbm, q_ref, q_sem)
    lens_copy = pltpu.make_async_copy(lens_hbm, lens_ref, lens_sem)

    def send(h, src, dst, s, r, device):
        return pltpu.make_async_remote_copy(
            src_ref=buf.at[h, src],
            dst_ref=buf.at[h, dst],
            send_sem=ssem.at[s],
            recv_sem=rsem.at[h, r],
            device_id=device,
            device_id_type=MESH,
        )

    def to_up(h):
        return send(h, block(0), block(BACK), 0, BACK, up)

    def to_right(h):
        return send(h, i + 8 * (1 - (x + 1) // ROW), block(1), 1, 1, right)

    def to_left(h):
        return send(h, i + 8 * ((ROW - 1 - x) // (ROW - 1)), block(3), 3, 3, left)

    def to_across(h):
        return send(h, i + 8 * (1 - x // 2), block(2), 2, 2, across)

    def share(h, slot):
        return send(h, block(slot), block(slot), 4 + slot, 5 + slot, partner)

    def arrived(h, slot):
        send(h, block(slot), block(slot), 0, slot, partner).wait_recv()

    def shared(h, slot):
        other = 2 * (BACK - slot) + 1 - i
        send(h, other, other, 0, 5 + slot, partner).wait_recv()

    def stage1(h):
        @pl.when(has_down)
        def _():
            arrived(h, 4)

        to_left(h).start()
        to_right(h).start()
        to_across(h).start()

        @pl.when(i == 1)
        def _():
            share(h, BACK).start()

    def stage2(h):
        for slot in (1, 3, 2):
            arrived(h, slot)
            share(h, slot).start()

    for h in range(KVH):
        own(h, 0).start()
        own(h, 1).start()
    lens_copy.start()
    barrier = pltpu.get_barrier_semaphore()
    for device in (left, right, across, partner):
        pl.semaphore_signal(barrier, inc=1, device_id=device, device_id_type=MESH)

    @pl.when(has_down)
    def _():
        pl.semaphore_signal(barrier, inc=1, device_id=down, device_id_type=MESH)

    @pl.when(has_up)
    def _():
        pl.semaphore_signal(barrier, inc=1, device_id=up, device_id_type=MESH)

    @pl.when(c < ROW)
    def _():
        for h in range(KVH):
            own(h, 0, BACK).start()
            own(h, 1, BACK).start()
        behind = buf.at[:, block(BACK)]
        pltpu.make_async_copy(behind, behind, fill_sem).wait()

    pl.semaphore_wait(barrier, 4 + jnp.minimum(c // ROW, 1) + jnp.minimum((n - 1 - c) // ROW, 1))
    for h in range(KVH):
        mine = buf.at[h, block(0)]
        pltpu.make_async_copy(mine, mine, kv_sem.at[h]).wait()

        @pl.when(has_up)
        def _():
            to_up(h).start()


    @pl.when(i == 0)
    def _():
        for h in range(KVH):
            share(h, 0).start()

    q_copy.start()

    lens_copy.wait()
    docs = lens_ref.shape[1]
    lens = lens_ref[...].astype(jnp.float32)
    ia = lax.broadcasted_iota(jnp.int32, (docs, docs), 0)
    ib = lax.broadcasted_iota(jnp.int32, (docs, docs), 1)
    column = jnp.sum(jnp.where(ia == ib, lens, 0.0), axis=1, keepdims=True)
    ends = jnp.sum(jnp.where(ia <= ib, column, 0.0), axis=0, keepdims=True)
    begin = c * (2 * T) + i * T - (WINDOW - 1) * T
    position = begin + lax.broadcasted_iota(jnp.int32, (WINDOW * T, 1), 0)
    before = (ends <= position.astype(jnp.float32)).astype(jnp.float32)
    doc = jnp.sum(before, axis=1, keepdims=True)
    doc = doc - doc[(WINDOW - 1) * T:(WINDOW - 1) * T + 1, :]
    lane = lax.broadcasted_iota(jnp.int32, (WINDOW * T, T), 1).astype(jnp.float32)
    same = (doc == lane) & (position >= 0)
    fk_ref[...] = jnp.where(same, 0.0, 1.0).astype(jnp.bfloat16)
    fq_ref[...] = jnp.where(same[(WINDOW - 1) * T:], -BIG, 0.0).astype(jnp.bfloat16)
    row = lax.broadcasted_iota(jnp.int32, (PAIR * T, T), 0) % T
    col = lax.broadcasted_iota(jnp.int32, (PAIR * T, T), 1)
    bias_ref[...] = jnp.where(col <= row, 0.0, -BIG)

    def compute(h):
        keys = buf[h, pl.ds(i, WINDOW), 0].reshape(WINDOW * T, HD)
        values = buf[h, pl.ds(i, WINDOW), 1].reshape(WINDOW * T, HD)
        keys = jnp.concatenate([keys, fk_ref[...]], axis=1)
        values = jnp.concatenate([values, jnp.ones((WINDOW * T, HD), jnp.bfloat16)], axis=1)
        factor = jnp.float32(HD**-0.5 * math.log2(math.e))
        for pair in range(GROUP // PAIR):
            at = [pl.multiple_of((h * GROUP + pair * PAIR + g) * HD, HD) for g in range(PAIR)]
            q = jnp.concatenate(
                [jnp.concatenate([q_ref[:, pl.ds(a, HD)], fq_ref[...]], axis=1) for a in at], axis=0
            )
            s = lax.dot_general(q, keys, (((1,), (1,)), ((), ())), preferred_element_type=jnp.float32)
            far, near = s[:, :(WINDOW - 1) * T], s[:, (WINDOW - 1) * T:] + bias_ref[...]
            s = jnp.concatenate([far, near], axis=1)
            top = jnp.max(s, axis=1, keepdims=True)
            w = jnp.exp2((s - top) * factor).astype(jnp.bfloat16)
            o = jnp.dot(w, values, preferred_element_type=jnp.float32)
            o = (o[:, :HD] / o[:, HD:]).astype(jnp.bfloat16)
            for g in range(PAIR):
                out_ref[:, pl.ds(at[g], HD)] = o[g * T:(g + 1) * T]

    for h in range(4):
        stage1(h)
    stage2(0)
    q_copy.wait()

    @pl.loop(0, KVH)
    def _(h):
        @pl.when(h + 4 < KVH)
        def _():
            stage1(h + 4)

        @pl.when(h + 1 < KVH)
        def _():
            stage2(h + 1)

        for slot in (1, 2, 3, BACK * (1 - i)):
            shared(h, slot)
        compute(h)

    def all_sent(sem):
        every = buf.at[:, block(0)]
        pltpu.make_async_remote_copy(
            src_ref=every,
            dst_ref=every,
            send_sem=ssem.at[sem],
            recv_sem=rsem.at[0, 0],
            device_id=partner,
            device_id_type=MESH,
        ).wait_send()

    @pl.when(has_up)
    def _():
        all_sent(0)

    for sem in (1, 2, 3, 5, 6, 7, 4 + BACK * i):
        all_sent(sem)


def per_device(queries, keys, values, doc_lengths):
    hbm = pl.BlockSpec(memory_space=pltpu.HBM)
    vmem = pl.BlockSpec(memory_space=pltpu.VMEM)
    lengths = doc_lengths.reshape(1, -1)
    operands = [pltpu.with_memory_space_constraint(a, pltpu.HBM) for a in (lengths, queries, keys, values)]
    return pl.pallas_call(
        kernel,
        out_shape=jax.ShapeDtypeStruct(queries.shape, queries.dtype),
        in_specs=[hbm, hbm, hbm, hbm],
        out_specs=vmem,
        scratch_shapes=[
            pltpu.VMEM((1, doc_lengths.shape[0]), jnp.int32),
            pltpu.VMEM((T, H * HD), jnp.bfloat16),
            pltpu.VMEM((KVH, BLOCKS, 2, T, HD), jnp.bfloat16),
            pltpu.VMEM((WINDOW * T, HD), jnp.bfloat16),
            pltpu.VMEM((T, HD), jnp.bfloat16),
            pltpu.VMEM((PAIR * T, T), jnp.float32),
            pltpu.SemaphoreType.DMA,
            pltpu.SemaphoreType.DMA,
            pltpu.SemaphoreType.DMA,
            pltpu.SemaphoreType.DMA((KVH,)),
            pltpu.SemaphoreType.DMA((9,)),
            pltpu.SemaphoreType.DMA((KVH, 10)),
        ],
        compiler_params=pltpu.CompilerParams(collective_id=0, has_side_effects=True, vmem_limit_bytes=24 << 20),
    )(*operands)


def solution(mesh):
    placed = (P(("ctx", "head"), None), P(("ctx", "head"), None), P(("ctx", "head"), None), P())
    return jax.shard_map(
        per_device, mesh=mesh, in_specs=placed, out_specs=P(("ctx", "head"), None), check_vma=False
    )
```

```python
import math

import jax
import jax.numpy as jnp
from jax import lax
from jax.experimental import pallas as pl
from jax.experimental.pallas import tpu as pltpu
from jax.sharding import PartitionSpec as P

H = 64
KVH = 8
HD = 128
GROUP = H // KVH
ROW = 4
BACK = 4
BLOCKS = 2 * (BACK + 1)
WINDOW = 2 * BACK + 1
T = 128
PAIR = 2
BIG = float(2**24)
MESH = pl.DeviceIdType.MESH


def kernel(
    lens_hbm, q_hbm, k_hbm, v_hbm, out_ref,
    lens_ref, q_ref, buf, fk_ref, fq_ref, bias_ref, lens_sem, q_sem, fill_sem, kv_sem, ssem, rsem,
):
    c = lax.axis_index("ctx")
    i = lax.axis_index("head")
    n = lax.axis_size("ctx")
    x = c % ROW
    first = (c // ROW) * ROW
    right = (first + (x + 1) % ROW, i)
    left = (first + (x + ROW - 1) % ROW, i)
    up = ((c + ROW) % n, i)
    down = ((c + n - ROW) % n, i)
    partner = (c, 1 - i)
    across = (first + (x + 2) % ROW, i)
    has_down = c >= ROW
    has_up = c < n - ROW

    def block(slot):
        return 2 * (BACK - slot) + i

    def own(h, which, slot=0):
        source = (k_hbm, v_hbm)[which].at[:, pl.ds(pl.multiple_of(h * HD, HD), HD)]
        return pltpu.make_async_copy(source, buf.at[h, block(slot), which], fill_sem if slot else kv_sem.at[h])

    q_copy = pltpu.make_async_copy(q_hbm, q_ref, q_sem)
    lens_copy = pltpu.make_async_copy(lens_hbm, lens_ref, lens_sem)

    def send(h, src, dst, s, r, device):
        return pltpu.make_async_remote_copy(
            src_ref=buf.at[h, src],
            dst_ref=buf.at[h, dst],
            send_sem=ssem.at[s],
            recv_sem=rsem.at[h, r],
            device_id=device,
            device_id_type=MESH,
        )

    def to_up(h):
        return send(h, block(0), block(BACK), 0, BACK, up)

    def to_right(h):
        return send(h, i + 8 * (1 - (x + 1) // ROW), block(1), 1, 1, right)

    def to_left(h):
        return send(h, i + 8 * ((ROW - 1 - x) // (ROW - 1)), block(3), 3, 3, left)

    def to_across(h):
        return send(h, i + 8 * (1 - x // 2), block(2), 2, 2, across)

    def share(h, slot):
        return send(h, block(slot), block(slot), 4 + slot, 5 + slot, partner)

    def arrived(h, slot):
        send(h, block(slot), block(slot), 0, slot, partner).wait_recv()

    def shared(h, slot):
        other = 2 * (BACK - slot) + 1 - i
        send(h, other, other, 0, 5 + slot, partner).wait_recv()

    def stage1(h):
        @pl.when(has_down)
        def _():
            arrived(h, 4)

        to_left(h).start()
        to_right(h).start()
        to_across(h).start()

        @pl.when(i == 1)
        def _():
            share(h, BACK).start()

    def stage2(h):
        for slot in (1, 3, 2):
            arrived(h, slot)
            share(h, slot).start()

    barrier = pltpu.get_barrier_semaphore()
    for device in (left, right, across, partner):
        pl.semaphore_signal(barrier, inc=1, device_id=device, device_id_type=MESH)

    @pl.when(has_down)
    def _():
        pl.semaphore_signal(barrier, inc=1, device_id=down, device_id_type=MESH)

    @pl.when(has_up)
    def _():
        pl.semaphore_signal(barrier, inc=1, device_id=up, device_id_type=MESH)

    for h in range(KVH):
        own(h, 0).start()
        own(h, 1).start()
    lens_copy.start()

    @pl.when(c < ROW)
    def _():
        for h in range(KVH):
            own(h, 0, BACK).start()
            own(h, 1, BACK).start()
        behind = buf.at[:, block(BACK)]
        pltpu.make_async_copy(behind, behind, fill_sem).wait()

    pl.semaphore_wait(barrier, 4 + jnp.minimum(c // ROW, 1) + jnp.minimum((n - 1 - c) // ROW, 1))
    for h in range(KVH):
        mine = buf.at[h, block(0)]
        pltpu.make_async_copy(mine, mine, kv_sem.at[h]).wait()

        @pl.when(has_up)
        def _():
            to_up(h).start()


    @pl.when(i == 0)
    def _():
        for h in range(KVH):
            share(h, 0).start()

    q_copy.start()

    lens_copy.wait()
    docs = lens_ref.shape[1]
    lens = lens_ref[...].astype(jnp.float32)
    ia = lax.broadcasted_iota(jnp.int32, (docs, docs), 0)
    ib = lax.broadcasted_iota(jnp.int32, (docs, docs), 1)
    column = jnp.sum(jnp.where(ia == ib, lens, 0.0), axis=1, keepdims=True)
    ends = jnp.sum(jnp.where(ia <= ib, column, 0.0), axis=0, keepdims=True)
    begin = c * (2 * T) + i * T - (WINDOW - 1) * T
    position = begin + lax.broadcasted_iota(jnp.int32, (WINDOW * T, 1), 0)
    before = (ends <= position.astype(jnp.float32)).astype(jnp.float32)
    doc = jnp.sum(before, axis=1, keepdims=True)
    doc = doc - doc[(WINDOW - 1) * T:(WINDOW - 1) * T + 1, :]
    lane = lax.broadcasted_iota(jnp.int32, (WINDOW * T, T), 1).astype(jnp.float32)
    same = (doc == lane) & (position >= 0)
    fk_ref[...] = jnp.where(same, 0.0, 1.0).astype(jnp.bfloat16)
    fq_ref[...] = jnp.where(same[(WINDOW - 1) * T:], -BIG, 0.0).astype(jnp.bfloat16)
    row = lax.broadcasted_iota(jnp.int32, (PAIR * T, T), 0) % T
    col = lax.broadcasted_iota(jnp.int32, (PAIR * T, T), 1)
    bias_ref[...] = jnp.where(col <= row, 0.0, -BIG)

    def compute(h):
        keys = buf[h, pl.ds(i, WINDOW), 0].reshape(WINDOW * T, HD)
        values = buf[h, pl.ds(i, WINDOW), 1].reshape(WINDOW * T, HD)
        keys = jnp.concatenate([keys, fk_ref[...]], axis=1)
        values = jnp.concatenate([values, jnp.ones((WINDOW * T, HD), jnp.bfloat16)], axis=1)
        factor = jnp.float32(HD**-0.5 * math.log2(math.e))
        for pair in range(GROUP // PAIR):
            at = [pl.multiple_of((h * GROUP + pair * PAIR + g) * HD, HD) for g in range(PAIR)]
            q = jnp.concatenate(
                [jnp.concatenate([q_ref[:, pl.ds(a, HD)], fq_ref[...]], axis=1) for a in at], axis=0
            )
            s = lax.dot_general(q, keys, (((1,), (1,)), ((), ())), preferred_element_type=jnp.float32)
            far, near = s[:, :(WINDOW - 1) * T], s[:, (WINDOW - 1) * T:] + bias_ref[...]
            s = jnp.concatenate([far, near], axis=1)
            top = jnp.max(s, axis=1, keepdims=True)
            w = jnp.exp2((s - top) * factor).astype(jnp.bfloat16)
            o = jnp.dot(w, values, preferred_element_type=jnp.float32)
            o = (o[:, :HD] / o[:, HD:]).astype(jnp.bfloat16)
            for g in range(PAIR):
                out_ref[:, pl.ds(at[g], HD)] = o[g * T:(g + 1) * T]

    for h in range(4):
        stage1(h)
    stage2(0)
    q_copy.wait()

    @pl.loop(0, KVH)
    def _(h):
        @pl.when(h + 4 < KVH)
        def _():
            stage1(h + 4)

        @pl.when(h + 1 < KVH)
        def _():
            stage2(h + 1)

        for slot in (1, 2, 3, BACK * (1 - i)):
            shared(h, slot)
        compute(h)

    def all_sent(sem):
        every = buf.at[:, block(0)]
        pltpu.make_async_remote_copy(
            src_ref=every,
            dst_ref=every,
            send_sem=ssem.at[sem],
            recv_sem=rsem.at[0, 0],
            device_id=partner,
            device_id_type=MESH,
        ).wait_send()

    @pl.when(has_up)
    def _():
        all_sent(0)

    for sem in (1, 2, 3, 5, 6, 7, 4 + BACK * i):
        all_sent(sem)


def per_device(queries, keys, values, doc_lengths):
    hbm = pl.BlockSpec(memory_space=pltpu.HBM)
    vmem = pl.BlockSpec(memory_space=pltpu.VMEM)
    lengths = doc_lengths.reshape(1, -1)
    operands = [pltpu.with_memory_space_constraint(a, pltpu.HBM) for a in (lengths, queries, keys, values)]
    return pl.pallas_call(
        kernel,
        out_shape=jax.ShapeDtypeStruct(queries.shape, queries.dtype),
        in_specs=[hbm, hbm, hbm, hbm],
        out_specs=vmem,
        scratch_shapes=[
            pltpu.VMEM((1, doc_lengths.shape[0]), jnp.int32),
            pltpu.VMEM((T, H * HD), jnp.bfloat16),
            pltpu.VMEM((KVH, BLOCKS, 2, T, HD), jnp.bfloat16),
            pltpu.VMEM((WINDOW * T, HD), jnp.bfloat16),
            pltpu.VMEM((T, HD), jnp.bfloat16),
            pltpu.VMEM((PAIR * T, T), jnp.float32),
            pltpu.SemaphoreType.DMA,
            pltpu.SemaphoreType.DMA,
            pltpu.SemaphoreType.DMA,
            pltpu.SemaphoreType.DMA((KVH,)),
            pltpu.SemaphoreType.DMA((9,)),
            pltpu.SemaphoreType.DMA((KVH, 10)),
        ],
        compiler_params=pltpu.CompilerParams(collective_id=0, has_side_effects=True, vmem_limit_bytes=24 << 20),
    )(*operands)


def solution(mesh):
    placed = (P(("ctx", "head"), None), P(("ctx", "head"), None), P(("ctx", "head"), None), P())
    return jax.shard_map(
        per_device, mesh=mesh, in_specs=placed, out_specs=P(("ctx", "head"), None), check_vma=False
    )
```
